1024 devices in a mesh: expert: 8 (over z), fsdp: 8 (over y), tensor: 16 (over x, core).
Axes of the slice: x: 8, y: 8, z: 8, core: 2. Of those that a mesh axis runs over, the one named last changes fastest.
Arguments:
- tokens: bfloat16 [1024, 4096], P('expert', 'tensor'), may hold values from -6 to 6
- expert_ids: int32 [1024, 2], P('expert'), may hold values from 0 to 7, all different within a row; in each aligned block of 128 rows (0 to 127, 128 to 255, ...) at most 48 rows name the same one
- gate_probs: float32 [1024, 2], P('expert'), may hold values from 0.1 to 1
- w_gate: bfloat16 [8, 4096, 14336], P('expert', 'tensor', 'fsdp'), may hold values from -0.09375 to 0.09375
- w_up: bfloat16 [8, 4096, 14336], P('expert', 'tensor', 'fsdp'), may hold values from -0.09375 to 0.09375
- w_down: bfloat16 [8, 14336, 4096], P('expert', 'fsdp', 'tensor'), may hold values from -0.046875 to 0.046875
Outputs:
- mixed: bfloat16 [1024, 4096], P('expert', 'tensor')
The draws below stay inside these ranges and needn't reach their ends.
Inputs may be any that keep to these rules, and one draw needn't show every extreme that they name: `expert_ids`: in each aligned block of 128 tokens no expert is named by more than 48 tokens, a bound that some block reaches; a token names two different experts.
All inputs are finite; a program needn't handle non-finite values.
Results may differ from the reference program's by a relative error of at most 0.0049.
Values may be sent and summed in bfloat16 or wider, within the bound.
A program may use at most 32 MiB of HBM per device.

```python
import math
import jax
import jax.numpy as jnp
import numpy as np
from jax import lax

D = 4096
FF = 14336
TOPK = 2
TOK_DEV = 128
EXPERTS = 8
CAP = 48
TOKENS = 1024


def levels(rng, dims, pieces, low, high):
    def one(dim, shards_of):
        steps = jax.random.uniform(jax.random.fold_in(jax.random.fold_in(rng, 6), dim), (shards_of,), jnp.float32, low / len(pieces), high / len(pieces))
        return jnp.repeat(jnp.exp(steps), dims[dim] // shards_of).reshape((-1,) + (1,) * (len(dims) - dim - 1))

    factor_of = one(*pieces[0])
    for cut in pieces[1:]:
        factor_of = factor_of * one(*cut)
    return factor_of


def routed_block(rng, own, number, rows, number_of, top, reach, skew):
    order = jax.random.permutation(rng, number_of)
    crowded, usual = shares(number_of, rows * top, reach, skew, True), shares(number_of, rows * top, reach, skew, False)
    places = jnp.arange(number_of)

    def named(tallies, rotation):
        used = int((tallies > 0).sum())
        fixed = max(1, used // 4)
        moved = fixed + (places - fixed + rotation * (used - fixed)) % max(1, number_of - fixed)
        return jnp.zeros((number_of,), jnp.int32).at[order[jnp.where(places < fixed, places, moved)]].set(jnp.asarray(tallies, jnp.int32))

    tallies = jnp.where(number % 4 == 0, named(crowded, number // 4), named(usual, number - number // 4 - 1))
    mixed = jax.random.permutation(jax.random.fold_in(own, 3), number_of)
    source_of, taker = mixed[0:number_of // 2 * 2:2], mixed[1:number_of // 2 * 2:2]
    room = jnp.minimum(tallies[source_of] - 1, reach - tallies[taker]) // 2
    room = jnp.where((source_of == order[0]) | (taker == order[0]) | (tallies[taker] == 0), 0, jnp.maximum(room, 0))
    moved = jax.random.randint(jax.random.fold_in(own, 4), (number_of // 2,), 0, 1 << 20) % (room + 1)
    tallies = tallies.at[source_of].add(-moved).at[taker].add(moved)
    labels = jnp.searchsorted(jnp.cumsum(tallies), jnp.arange(rows * top), side="right").astype(jnp.int32)
    grid = labels.reshape(top, rows).T
    grid = grid[jax.random.permutation(jax.random.fold_in(own, 1), rows)]
    rotation = jax.random.randint(jax.random.fold_in(own, 2), (rows, 1), 0, top)
    return jnp.take_along_axis(grid, (jnp.arange(top)[None, :] + rotation) % top, axis=1)


def shares(amount, total, bound, skew, full):
    portions = [(1 << 20) // math.isqrt(standing ** skew) + 1 for standing in range(1, amount + 1)]
    largest = bound if full else min(bound, max(-(-total // amount), total * portions[0] // sum(portions)))
    least = 1 if total - largest >= amount - 1 else 0
    given, surplus = [largest] + [least] * (amount - 1), total - largest - least * (amount - 1)
    while surplus > 0:
        candidates = [i for i in range(1, amount) if given[i] < largest] or [i for i in range(1, amount) if given[i] < bound]
        whole, left = sum([portions[i] for i in candidates]), surplus
        for i in candidates:
            addition = min(bound - given[i], max(1, left * portions[i] // whole), surplus)
            given[i] = given[i] + addition
            surplus = surplus - addition
    return np.array(given)


def normal_values(rng, dims, spread, bound, cuts=(), held_as=jnp.bfloat16):
    loudness = levels(rng, dims, cuts, -0.22, 0.18) if cuts else 1.0
    array = jax.random.normal(rng, dims, jnp.float32) * spread * loudness
    return jnp.minimum(jnp.maximum(array, -bound), bound).astype(held_as)


def setup_inputs(seed: int = 0) -> dict:
    key_list = jax.random.split(jax.random.key(seed), 7)
    tokens = normal_values(key_list[0], (TOKENS, D), 1.0, 6.0, ((0, 8), (1, 16)))
    expert_ids_keys = jax.random.split(jax.random.fold_in(key_list[1], 1), TOKENS // TOK_DEV)
    expert_ids_turns = jax.random.permutation(jax.random.fold_in(key_list[1], 3), TOKENS // TOK_DEV)
    expert_ids = jax.vmap(lambda own, number: routed_block(jax.random.fold_in(key_list[1], 2), own, number, TOK_DEV, EXPERTS, TOPK, CAP, 2))(expert_ids_keys, expert_ids_turns).reshape((TOKENS, TOPK))
    gate_probs = jnp.clip(0.1 + 0.9 * jax.random.uniform(key_list[2], (TOKENS, TOPK), jnp.float32) ** levels(key_list[2], (TOKENS, TOPK), ((0, 8),), -0.2, 0.2), 0.1, 1.0)
    w_gate = normal_values(key_list[3], (EXPERTS, D, FF), D ** -0.5, 0.09375, ((0, 8), (1, 16), (2, 8)))
    w_up = normal_values(key_list[4], (EXPERTS, D, FF), D ** -0.5, 0.09375, ((0, 8), (1, 16), (2, 8)))
    w_down = normal_values(key_list[5], (EXPERTS, FF, D), FF ** -0.5, 0.046875, ((0, 8), (1, 8), (2, 16)))
    return dict(tokens=tokens, expert_ids=expert_ids, gate_probs=gate_probs, w_gate=w_gate, w_up=w_up, w_down=w_down)


def expert_apply(operands):
    rows_in, gate_matrix, up_matrix, down_matrix = operands
    gate = jnp.dot(rows_in, gate_matrix, preferred_element_type=jnp.float32)
    up_value = jnp.dot(rows_in, up_matrix, preferred_element_type=jnp.float32)
    hidden = (jax.nn.silu(gate) * up_value).astype(jnp.bfloat16)
    return jnp.dot(hidden, down_matrix, preferred_element_type=jnp.float32)


def reference(tokens, expert_ids, gate_probs, w_gate, w_up, w_down):
    sources = TOKENS // TOK_DEV
    block_ids = expert_ids.reshape(sources, TOK_DEV * TOPK)
    onehot = (block_ids[:, :, None] == jnp.arange(EXPERTS, dtype=jnp.int32)[None, None, :]).astype(jnp.int32)
    slot_rank = jnp.cumsum(onehot, axis=1) - onehot
    slot_index = jnp.sum(slot_rank * onehot, axis=2).astype(jnp.int32)
    row_index = (jnp.arange(sources, dtype=jnp.int32)[:, None] * CAP + slot_index).astype(jnp.int32)
    doubled = jnp.repeat(tokens.reshape(sources, TOK_DEV, D), TOPK, axis=1)
    dispatched = jnp.zeros((EXPERTS, sources * CAP, D), jnp.bfloat16)
    dispatched = dispatched.at[block_ids, row_index].set(doubled)
    expert_out = lax.map(expert_apply, (dispatched, w_gate, w_up, w_down))
    picked = expert_out[block_ids, row_index]
    picked = picked.reshape(sources, TOK_DEV, TOPK, D)
    weights = gate_probs.reshape(sources, TOK_DEV, TOPK, 1)
    mixed = jnp.sum(picked * weights, axis=2)
    return mixed.reshape(TOKENS, D).astype(jnp.bfloat16)
```

```python
import functools

import jax
import jax.numpy as jnp
from jax import lax
from jax.experimental import pallas as pl
from jax.experimental.pallas import tpu as pltpu
from jax.sharding import PartitionSpec as P

MESH = pl.DeviceIdType.MESH
CH = 16
BF = jnp.bfloat16
F32 = jnp.float32


def block_order(n):
    order = [0]
    for d in range(1, n // 2 + 1):
        order.append(d)
        if d != n - d:
            order.append(n - d)
    return order


def kernel(
    cfg,
    tok_hbm, ids_hbm, prob_hbm, wg_hbm, wu_hbm, wd_hbm, out_ref,
    tok, ids, prob, wgu, wd, outg, comb, xs, part, sf, sb, sl, rf, rb, rl, hid, osb, ret, mix, yrecv, yown, res,
    ld_sem, w_ss, w_rs, d_ss, d_rs, f_ss, f_rs, r_ss, r_rs, a_ss, a_rs, h_ss, h_rs, o_ss, o_rs, y1_ss, y1_rs, y2_ss, y2_rs,
):
    ne, nf, nx, cap = cfg["ne"], cfg["nf"], cfg["nx"], cfg["cap"]
    half, lag = cfg["half"], cfg["lag"]
    order = block_order(ne)
    per = cap // CH
    groups = ne * per // nx
    fwd_n, bwd_n = nx // 2, nx - 1 - nx // 2
    tokens_n = tok.shape[0]
    feat = tok.shape[1]

    z, y, t = lax.axis_index("expert"), lax.axis_index("fsdp"), lax.axis_index("tensor")
    x, c = t // 2, t % 2
    other = 1 - c
    sgn = 1 - 2 * c
    partner = (z, y, x * 2 + other)

    def at_x(k):
        return (x + sgn * k + 2 * nx) % nx

    def dev_x(k):
        return (z, y, at_x(k) * 2 + c)

    def dev_z(k):
        return ((z + k + ne) % ne, y, t)

    def dev_y(k):
        return (z, (y + k + nf) % nf, t)

    def remote(src, dst, ss, rs, dev):
        return pltpu.make_async_remote_copy(
            src_ref=src, dst_ref=dst, send_sem=ss, recv_sem=rs, device_id=dev, device_id_type=MESH
        )

    sends = []

    mine = pl.ds(pl.multiple_of(c * half, 128), half)
    theirs = pl.ds(pl.multiple_of(other * half, 128), half)
    loads = [
        pltpu.make_async_copy(ids_hbm, ids, ld_sem.at[0]),
        pltpu.make_async_copy(prob_hbm, prob, ld_sem.at[1]),
        pltpu.make_async_copy(tok_hbm, tok, ld_sem.at[2]),
        pltpu.make_async_copy(wg_hbm.at[:, mine], wgu.at[c, :, 0:half], ld_sem.at[3]),
        pltpu.make_async_copy(wu_hbm.at[:, mine], wgu.at[c, :, half : 2 * half], ld_sem.at[4]),
        pltpu.make_async_copy(wd_hbm, wd, ld_sem.at[5]),
    ]
    for copy in loads:
        copy.start()

    barrier = pltpu.get_barrier_semaphore()
    peers = [partner]
    if nx > 1:
        peers.append(dev_x(1))
        if nx > 2:
            peers.append(dev_x(-1))
    peers += [dev_z(k) for k in range(1, ne)]
    peers += [dev_y(k) for k in range(1, nf)]
    for peer in peers:
        pl.semaphore_signal(barrier, inc=1, device_id=peer, device_id_type=MESH)

    loads[0].wait()
    loads[1].wait()
    expert_row = lax.broadcasted_iota(jnp.int32, (ne, tokens_n), 0)
    first = expert_row == ids[0:1, :]
    second = expert_row == ids[1:2, :]
    named = jnp.where(first, 1.0, 0.0) + jnp.where(second, 1.0, 0.0)
    weight = jnp.where(first, prob[0:1, :], 0.0) + jnp.where(second, prob[1:2, :], 0.0)
    earlier = jnp.where(
        lax.broadcasted_iota(jnp.int32, (tokens_n, tokens_n), 0)
        < lax.broadcasted_iota(jnp.int32, (tokens_n, tokens_n), 1),
        1.0,
        0.0,
    ).astype(BF)
    rank = jnp.dot(named.astype(BF), earlier, preferred_element_type=F32)
    rank = jnp.where(named > 0.5, rank, -1.0)
    slot_row = lax.broadcasted_iota(jnp.int32, (cap, tokens_n), 0).astype(F32)
    loads[2].wait()
    for e in range(ne):
        chosen = slot_row == rank[e : e + 1, :]
        rows = jnp.dot(jnp.where(chosen, 1.0, 0.0).astype(BF), tok[...], preferred_element_type=F32)
        outg[e] = rows.astype(BF).reshape(per, CH, feat)
        comb[e * cap : (e + 1) * cap, :] = jnp.where(chosen, weight[e : e + 1, :], 0.0)

    pl.semaphore_wait(barrier, len(peers))

    swaps = [
        remote(wg_hbm.at[:, theirs], wgu.at[c, :, 0:half], w_ss.at[0], w_rs.at[0], partner),
        remote(wu_hbm.at[:, theirs], wgu.at[c, :, half : 2 * half], w_ss.at[1], w_rs.at[1], partner),
    ]
    for copy in swaps:
        copy.start()
        sends.append(copy)

    xs[c, 0:per] = outg[z]
    dispatch = [None]
    for p in range(1, ne):
        copy = remote(
            outg.at[(z - order[p] + ne) % ne], xs.at[c, p * per : (p + 1) * per], d_ss.at[p], d_rs.at[p], dev_z(-order[p])
        )
        copy.start()
        dispatch.append(copy)
        sends.append(copy)

    handed = {}

    def hand(p):
        if p in handed:
            return
        if p > 0:
            dispatch[p].wait_recv()
        view = xs.at[c, p * per : (p + 1) * per]
        copy = remote(view, view, f_ss.at[p], f_rs.at[p], partner)
        copy.start()
        handed[p] = copy
        sends.append(copy)

    def blocks_of(g):
        return range(g * nx // per, ((g + 1) * nx - 1) // per + 1)

    taken = set()
    loaded = []

    def first_product(g):
        for p in blocks_of(g):
            hand(p)
        if not loaded:
            for copy in (loads[3], loads[4]):
                copy.wait()
            for copy in swaps:
                copy.wait_recv()
            loaded.append(1)
        for p in blocks_of(g):
            if p not in taken:
                handed[p].wait_recv()
                taken.add(p)
        a0 = xs[0, g * nx : (g + 1) * nx].reshape(nx * CH, feat)
        a1 = xs[1, g * nx : (g + 1) * nx].reshape(nx * CH, feat)
        tile = cfg["tile"]
        for n in range(2 * half // tile):
            cols = slice(n * tile, (n + 1) * tile)
            acc = jnp.dot(a0, wgu[0, :, cols], preferred_element_type=F32)
            acc += jnp.dot(a1, wgu[1, :, cols], preferred_element_type=F32)
            part[g * nx : (g + 1) * nx, :, cols] = acc.reshape(nx, CH, tile)

    reduce_f, reduce_b = {}, {}

    def reduce_step(g, k):
        if k < fwd_n:
            value = part[g * nx + at_x(fwd_n - k)]
            if k > 0:
                reduce_f[g, k - 1].wait_recv()
                value = value + rf[g, k - 1].astype(F32)
            i = g * (nx - 1) + k
            if k < fwd_n - 1:
                sf[g, k] = value.astype(BF)
                copy = remote(sf.at[g, k], rf.at[g, k], r_ss.at[i], r_rs.at[i], dev_x(1))
            else:
                sl[g] = value
                copy = remote(sl.at[g], rl.at[g], r_ss.at[i], r_rs.at[i], dev_x(1))
            copy.start()
            reduce_f[g, k] = copy
            sends.append(copy)
        if k < bwd_n:
            value = part[g * nx + at_x(-(bwd_n - k))]
            if k > 0:
                reduce_b[g, k - 1].wait_recv()
                value = value + rb[g, k - 1].astype(F32)
            sb[g, k] = value.astype(BF)
            i = g * (nx - 1) + fwd_n + k
            copy = remote(sb.at[g, k], rb.at[g, k], r_ss.at[i], r_rs.at[i], dev_x(-1))
            copy.start()
            reduce_b[g, k] = copy
            sends.append(copy)

    given = {}

    def give(g, owner, n):
        view = hid.at[c, g * nx + owner]
        i = g * nx + n
        copy = remote(view, view, h_ss.at[i], h_rs.at[i], partner)
        copy.start()
        given[g, n] = copy
        sends.append(copy)

    gather_f, gather_b = {}, {}
    gf_n, gb_n = bwd_n, fwd_n

    def finish(g):
        value = part[g * nx + x]
        if fwd_n:
            reduce_f[g, fwd_n - 1].wait_recv()
            value = value + rl[g]
        if bwd_n:
            reduce_b[g, bwd_n - 1].wait_recv()
            value = value + rb[g, bwd_n - 1].astype(F32)
        gate, up = value[:, :half], value[:, half:]
        hid[c, g * nx + x] = (gate / (1.0 + jnp.exp(-gate)) * up).astype(BF)
        gather_step(g, 0)

    def gather_step(g, k):
        if k <= gf_n:
            owner = at_x(-k)
            if k > 0:
                gather_f[g, k - 1].wait_recv()
            if k < gf_n:
                view = hid.at[c, g * nx + owner]
                i = g * (nx - 1) + k
                copy = remote(view, view, a_ss.at[i], a_rs.at[i], dev_x(1))
                copy.start()
                gather_f[g, k] = copy
                sends.append(copy)
            if k > 0:
                give(g, owner, k)
        if k <= gb_n:
            owner = at_x(k)
            if k > 0:
                gather_b[g, k - 1].wait_recv()
            if k < gb_n:
                view = hid.at[c, g * nx + owner]
                i = g * (nx - 1) + gf_n + k
                copy = remote(view, view, a_ss.at[i], a_rs.at[i], dev_x(-1))
                copy.start()
                gather_b[g, k] = copy
                sends.append(copy)
            if k > 0:
                give(g, owner, gf_n + k)
        if k == 0:
            give(g, x, 0)

    returns = []

    def second_product(g):
        if g == 0:
            loads[5].wait()
        for n in range(nx):
            given[g, n].wait_recv()
        h0 = hid[0, g * nx : (g + 1) * nx].reshape(nx * CH, half)
        h1 = hid[1, g * nx : (g + 1) * nx].reshape(nx * CH, half)
        value = jnp.dot(h0, wd[0:half, :], preferred_element_type=F32)
        value += jnp.dot(h1, wd[half : 2 * half, :], preferred_element_type=F32)
        osb[g * nx : (g + 1) * nx] = value.reshape(nx, CH, feat)
        at = g * nx
        while at < (g + 1) * nx:
            p = at // per
            end = min((p + 1) * per, (g + 1) * nx)
            lo, hi_ = at - p * per, end - p * per
            if p == 0:
                ret[z, lo:hi_] = osb[at:end]
            else:
                i = len(returns)
                copy = remote(
                    osb.at[at:end], ret.at[z, lo:hi_], o_ss.at[i], o_rs.at[i], dev_z(order[p])
                )
                copy.start()
                returns.append(copy)
                sends.append(copy)
            at = end

    stages = [lambda g: (first_product(g), reduce_step(g, 0))]
    for k in range(1, fwd_n):
        stages.append(functools.partial(lambda k, g: reduce_step(g, k), k))
    stages.append(finish)
    for k in range(1, max(gf_n, gb_n) + 1):
        stages.append(functools.partial(lambda k, g: gather_step(g, k), k))
    stages.append(second_product)
    for slot in range(len(stages) + lag * (groups - 1)):
        for g in range(groups):
            if 0 <= slot - lag * g < len(stages):
                stages[slot - lag * g](g)

    for copy in returns:
        copy.wait_recv()
    rows = ret[...].reshape(ne * cap, feat)
    total = lax.dot_general(
        comb[...], rows, (((0,), (0,)), ((), ())), preferred_element_type=F32, precision=lax.Precision.HIGHEST
    )
    piece = tokens_n // nf
    mix[...] = total.reshape(nf, piece, feat)
    first_y, second_y = [], []
    for k in range(1, nf):
        copy = remote(mix.at[(y + k) % nf], yrecv.at[k], y1_ss.at[k], y1_rs.at[k], dev_y(k))
        copy.start()
        first_y.append(copy)
        sends.append(copy)
    value = mix[y]
    for k in range(1, nf):
        first_y[k - 1].wait_recv()
        value = value + yrecv[k]
    yown[...] = value.astype(BF)
    res[y] = yown[...]
    for k in range(1, nf):
        copy = remote(yown, res.at[y], y2_ss.at[k], y2_rs.at[k], dev_y(k))
        copy.start()
        second_y.append(copy)
        sends.append(copy)
    for copy in second_y:
        copy.wait_recv()
    out_ref[...] = res[...].reshape(tokens_n, feat)
    for copy in sends:
        copy.wait_send()


def solution(mesh):
    ne, nf, nt = mesh.shape["expert"], mesh.shape["fsdp"], mesh.shape["tensor"]
    nx = nt // 2

    def body(tokens, expert_ids, gate_probs, w_gate, w_up, w_down):
        rows, feat = tokens.shape
        width = w_gate.shape[2]
        half = width // 2
        cap = 3 * rows // ne
        per = cap // CH
        chunks = ne * per
        groups = chunks // nx
        fwd_n, bwd_n = nx // 2, nx - 1 - nx // 2
        cfg = dict(ne=ne, nf=nf, nx=nx, cap=cap, half=half, lag=1, tile=256 if width % 256 == 0 else 128)
        any_ = pl.BlockSpec(memory_space=pl.ANY)
        dma = pltpu.SemaphoreType.DMA
        segments = chunks
        call = pl.pallas_call(
            functools.partial(kernel, cfg),
            out_shape=jax.ShapeDtypeStruct((rows, feat), BF),
            in_specs=[any_] * 6,
            out_specs=pl.BlockSpec(memory_space=pltpu.VMEM),
            scratch_shapes=[
                pltpu.VMEM((rows, feat), BF),
                pltpu.VMEM((2, rows), jnp.int32),
                pltpu.VMEM((2, rows), F32),
                pltpu.VMEM((2, feat, width), BF),
                pltpu.VMEM((width, feat), BF),
                pltpu.VMEM((ne, per, CH, feat), BF),
                pltpu.VMEM((ne * cap, rows), F32),
                pltpu.VMEM((2, chunks, CH, feat), BF),
                pltpu.VMEM((chunks, CH, width), F32),
                pltpu.VMEM((groups, max(fwd_n - 1, 1), CH, width), BF),
                pltpu.VMEM((groups, max(bwd_n, 1), CH, width), BF),
                pltpu.VMEM((groups, CH, width), F32),
                pltpu.VMEM((groups, max(fwd_n - 1, 1), CH, width), BF),
                pltpu.VMEM((groups, max(bwd_n, 1), CH, width), BF),
                pltpu.VMEM((groups, CH, width), F32),
                pltpu.VMEM((2, chunks, CH, half), BF),
                pltpu.VMEM((chunks, CH, feat), F32),
                pltpu.VMEM((ne, per, CH, feat), F32),
                pltpu.VMEM((nf, rows // nf, feat), F32),
                pltpu.VMEM((nf, rows // nf, feat), F32),
                pltpu.VMEM((rows // nf, feat), BF),
                pltpu.VMEM((nf, rows // nf, feat), BF),
                dma((6,)),
                dma((2,)), dma((2,)),
                dma((ne,)), dma((ne,)),
                dma((ne,)), dma((ne,)),
                dma((groups * (nx - 1),)), dma((groups * (nx - 1),)),
                dma((groups * (nx - 1),)), dma((groups * (nx - 1),)),
                dma((groups * nx,)), dma((groups * nx,)),
                dma((segments,)), dma((segments,)),
                dma((nf,)), dma((nf,)),
                dma((nf,)), dma((nf,)),
            ],
            compiler_params=pltpu.CompilerParams(
                collective_id=0, has_side_effects=True, vmem_limit_bytes=60 << 20
            ),
        )
        return call(tokens, expert_ids.T, gate_probs.T, w_gate[0], w_up[0], w_down[0])

    return jax.shard_map(
        body,
        mesh=mesh,
        in_specs=(
            P("expert", "tensor"),
            P("expert", None),
            P("expert", None),
            P("expert", "tensor", "fsdp"),
            P("expert", "tensor", "fsdp"),
            P("expert", "fsdp", "tensor"),
        ),
        out_specs=P("expert", "tensor"),
        check_vma=False,
    )
```

```python
import functools

import jax
import jax.numpy as jnp
from jax import lax
from jax.experimental import pallas as pl
from jax.experimental.pallas import tpu as pltpu
from jax.sharding import PartitionSpec as P

MESH = pl.DeviceIdType.MESH
CH = 16
BF = jnp.bfloat16
F32 = jnp.float32


def kernel(
    cfg,
    tok_hbm, ids_hbm, prob_hbm, wg_hbm, wu_hbm, wd_hbm, out_ref,
    tok, ids, prob, wgu, wd, outg, comb, xs, part, sb, rb, hid, osb, ret, yrecv, fin,
    ld_sem, w_ss, w_rs, d_ss, d_rs, f_ss, f_rs, r_ss, r_rs, a_ss, a_rs, h_ss, h_rs, y1_ss, y1_rs, y2_ss, y2_rs,
):
    ne, nf, nx, cap = cfg["ne"], cfg["nf"], cfg["nx"], cfg["cap"]
    half, lag = cfg["half"], cfg["lag"]
    per = cap // CH
    groups = ne * per // nx
    rows_y = nx * CH // nf
    in_block = cap // rows_y
    routes = []
    for way, reach in ((1, nx // 2), (-1, nx - 1 - nx // 2)):
        for d in range(reach, 1, -2):
            routes += [(way, d, "leaf"), (way, d - 1, "relay")]
        if reach % 2:
            routes.append((way, 1, "alone"))
    tokens_n = tok.shape[0]
    feat = tok.shape[1]

    z, y, t = lax.axis_index("expert"), lax.axis_index("fsdp"), lax.axis_index("tensor")
    x, c = t // 2, t % 2
    other = 1 - c
    sgn = 1 - 2 * c
    partner = (z, y, x * 2 + other)

    def at_x(k):
        return (x + sgn * k + 2 * nx) % nx

    def dev_x(k):
        return (z, y, at_x(k) * 2 + c)

    def dev_z(k):
        return ((z + k + ne) % ne, y, t)

    def dev_y(k):
        return (z, (y + k + nf) % nf, t)

    class Remote:
        def __init__(self, src, dst, ss, rs, dev):
            self.copy = pltpu.make_async_remote_copy(
                src_ref=src, dst_ref=dst, send_sem=ss, recv_sem=rs, device_id=dev, device_id_type=MESH
            )
            self.start, self.wait_send, self.waited = self.copy.start, self.copy.wait_send, False

        def wait_recv(self):
            if not self.waited:
                self.copy.wait_recv()
            self.waited = True

    remote = Remote
    sends = []

    mine = pl.ds(pl.multiple_of(c * half, 128), half)
    theirs = pl.ds(pl.multiple_of(other * half, 128), half)
    loads = [
        pltpu.make_async_copy(ids_hbm, ids, ld_sem.at[0]),
        pltpu.make_async_copy(prob_hbm, prob, ld_sem.at[1]),
        pltpu.make_async_copy(tok_hbm, tok, ld_sem.at[2]),
        pltpu.make_async_copy(wg_hbm.at[:, mine], wgu.at[c, :, 0:half], ld_sem.at[3]),
        pltpu.make_async_copy(wu_hbm.at[:, mine], wgu.at[c, :, half : 2 * half], ld_sem.at[4]),
        pltpu.make_async_copy(wd_hbm, wd, ld_sem.at[5]),
    ]
    for copy in loads:
        copy.start()

    barrier = pltpu.get_barrier_semaphore()
    peers = [partner]
    offsets = {way * d % nx for way, d, kind in routes if kind != "leaf"} | {way % nx for way, d, kind in routes}
    peers += [dev_x(k) for k in sorted(offsets | {-k % nx for k in offsets})]
    peers += [dev_z(k) for k in range(1, ne)]
    peers += [dev_y(k) for k in range(1, nf)]
    for peer in peers:
        pl.semaphore_signal(barrier, inc=1, device_id=peer, device_id_type=MESH)

    loads[0].wait()
    loads[1].wait()
    expert_row = lax.broadcasted_iota(jnp.int32, (ne, tokens_n), 0)
    first = expert_row == ids[0:1, :]
    second = expert_row == ids[1:2, :]
    named = jnp.where(first, 1.0, 0.0) + jnp.where(second, 1.0, 0.0)
    weight = jnp.where(first, prob[0:1, :], 0.0) + jnp.where(second, prob[1:2, :], 0.0)
    earlier = jnp.where(
        lax.broadcasted_iota(jnp.int32, (tokens_n, tokens_n), 0)
        < lax.broadcasted_iota(jnp.int32, (tokens_n, tokens_n), 1),
        1.0,
        0.0,
    ).astype(BF)
    rank = jnp.dot(named.astype(BF), earlier, preferred_element_type=F32)
    rank = jnp.where(named > 0.5, rank, -1.0)
    slot_row = lax.broadcasted_iota(jnp.int32, (cap, tokens_n), 0).astype(F32)
    hi = weight.astype(BF).astype(F32)
    mid = (weight - hi).astype(BF).astype(F32)
    low = weight - hi - mid
    loads[2].wait()
    for e in range(ne):
        chosen = slot_row == rank[e : e + 1, :]
        rows = jnp.dot(jnp.where(chosen, 1.0, 0.0).astype(BF), tok[...], preferred_element_type=F32)
        outg[e] = rows.astype(BF).reshape(per, CH, feat)
        for i, term in enumerate((hi, mid, low)):
            comb[i, e * cap : (e + 1) * cap, :] = jnp.where(chosen, term[e : e + 1, :], 0.0).astype(BF)

    pl.semaphore_wait(barrier, len(peers))

    swaps = [
        remote(wg_hbm.at[:, theirs], wgu.at[c, :, 0:half], w_ss.at[0], w_rs.at[0], partner),
        remote(wu_hbm.at[:, theirs], wgu.at[c, :, half : 2 * half], w_ss.at[1], w_rs.at[1], partner),
    ]
    for copy in swaps:
        copy.start()
        sends.append(copy)

    xs[c, 0:per] = outg[z]
    dispatch = [None]
    for p in range(1, ne):
        copy = remote(
            outg.at[(z - p + ne) % ne], xs.at[c, p * per : (p + 1) * per], d_ss.at[p], d_rs.at[p], dev_z(-p)
        )
        copy.start()
        dispatch.append(copy)
        sends.append(copy)

    handed = {}

    def hand(p):
        if p in handed:
            return
        if p > 0:
            dispatch[p].wait_recv()
        view = xs.at[c, p * per : (p + 1) * per]
        copy = remote(view, view, f_ss.at[p], f_rs.at[p], partner)
        copy.start()
        handed[p] = copy
        sends.append(copy)

    def blocks_of(g):
        return range(g * nx // per, ((g + 1) * nx - 1) // per + 1)

    taken = set()
    loaded = []

    def first_product(g):
        for p in blocks_of(g):
            hand(p)
        if not loaded:
            for copy in (loads[3], loads[4]):
                copy.wait()
            for copy in swaps:
                copy.wait_recv()
            loaded.append(1)
        for p in blocks_of(g):
            if p not in taken:
                handed[p].wait_recv()
                taken.add(p)
        a0 = xs[0, g * nx : (g + 1) * nx].reshape(nx * CH, feat)
        a1 = xs[1, g * nx : (g + 1) * nx].reshape(nx * CH, feat)
        tile = cfg["tile"]
        for n in range(2 * half // tile):
            cols = slice(n * tile, (n + 1) * tile)
            acc = jnp.dot(a0, wgu[0, :, cols], preferred_element_type=F32)
            acc += jnp.dot(a1, wgu[1, :, cols], preferred_element_type=F32)
            part[g * nx : (g + 1) * nx, :, cols] = acc.reshape(nx, CH, tile)

    got = {}

    def leaf_sends(g):
        for i, (way, d, kind) in enumerate(routes):
            if kind == "relay":
                continue
            sb[g, i] = part[g * nx + at_x(way * d)].astype(BF)
            j = g * (nx - 1) + i
            copy = remote(sb.at[g, i], rb.at[g, i], r_ss.at[j], r_rs.at[j], dev_x(way))
            copy.start()
            got[g, i] = copy
            sends.append(copy)

    def relay_sends(g):
        for i, (way, d, kind) in enumerate(routes):
            if kind != "relay":
                continue
            k = routes.index((way, d + 1, "leaf"))
            value = part[g * nx + at_x(way * d)]
            got[g, k].wait_recv()
            sb[g, i] = (value + rb[g, k].astype(F32)).astype(BF)
            j = g * (nx - 1) + i
            copy = remote(sb.at[g, i], rb.at[g, i], r_ss.at[j], r_rs.at[j], dev_x(way * d))
            copy.start()
            got[g, i] = copy
            sends.append(copy)

    given = {}

    def give(g, owner, n):
        view = hid.at[c, g * nx + owner]
        i = g * nx + n
        copy = remote(view, view, h_ss.at[i], h_rs.at[i], partner)
        copy.start()
        given[g, n] = copy
        sends.append(copy)

    def finish(g):
        value = part[g * nx + x]
        for i, (way, d, kind) in enumerate(routes):
            if kind != "leaf":
                got[g, i].wait_recv()
                value = value + rb[g, i].astype(F32)
        gate, up = value[:, :half], value[:, half:]
        hid[c, g * nx + x] = (gate / (1.0 + jnp.exp(-gate)) * up).astype(BF)
        for i, (way, d, kind) in enumerate(routes):
            if kind != "leaf":
                spread(g, i, x, way * d)
        give(g, x, nx - 1)

    shared = {}

    def spread(g, i, owner, to):
        view = hid.at[c, g * nx + owner]
        j = g * (nx - 1) + i
        copy = remote(view, view, a_ss.at[j], a_rs.at[j], dev_x(to))
        copy.start()
        shared[g, i] = copy
        sends.append(copy)

    def relay_hidden(g):
        for i, (way, d, kind) in enumerate(routes):
            if kind == "leaf":
                continue
            shared[g, i].wait_recv()
            owner = at_x(-way * d)
            if kind == "relay":
                spread(g, routes.index((way, d + 1, "leaf")), owner, way)
            give(g, owner, i)

    def collect_hidden(g):
        for i, (way, d, kind) in enumerate(routes):
            if kind == "leaf":
                shared[g, i].wait_recv()
                give(g, at_x(-way * d), i)

    summed, cast = {}, {}

    def second_product(g):
        if g == 0:
            loads[5].wait()
        for n in range(nx):
            given[g, n].wait_recv()
        h0 = hid[0, g * nx : (g + 1) * nx].reshape(nx * CH, half)
        h1 = hid[1, g * nx : (g + 1) * nx].reshape(nx * CH, half)
        value = jnp.dot(h0, wd[0:half, :], preferred_element_type=F32)
        value += jnp.dot(h1, wd[half : 2 * half, :], preferred_element_type=F32)
        osb[g] = value.reshape(nf, rows_y, feat)
        for k in range(1, nf):
            i = g * nf + k
            copy = remote(osb.at[g, (y + k) % nf], yrecv.at[g, k], y1_ss.at[i], y1_rs.at[i], dev_y(k))
            copy.start()
            summed[g, k] = copy
            sends.append(copy)

    def send_back(g):
        value = osb[g, y]
        for k in range(1, nf):
            summed[g, k].wait_recv()
            value = value + yrecv[g, k]
        fin[g] = value.astype(BF)
        q = g * nf + y
        home = q // in_block
        place = ret.at[z, q % in_block]
        to_z = (z + home) % ne
        for k in range(nf):
            i = g * nf + k
            copy = remote(fin.at[g], place, y2_ss.at[i], y2_rs.at[q], (to_z, (y + k) % nf, t))
            if k == 0 and g * nf < in_block:
                kept = q < in_block

                @pl.when(kept)
                def _():
                    ret[z, q % in_block] = fin[g]

                @pl.when(jnp.logical_not(kept))
                def _():
                    copy.start()

                own_sends.append((kept, copy))
            else:
                copy.start()
                sends.append(copy)

    own_sends = []
    stages = [
        lambda g: (first_product(g), leaf_sends(g)), relay_sends, finish, relay_hidden, collect_hidden, second_product, send_back,
    ]
    for slot in range(len(stages) + lag * (groups - 1)):
        for g in range(groups):
            if 0 <= slot - lag * g < len(stages):
                stages[slot - lag * g](g)

    for q in range(groups * nf):
        copy = remote(fin.at[0], ret.at[0, 0], y2_ss.at[0], y2_rs.at[q], partner)
        if q < in_block:

            @pl.when(y != q % nf)
            def _():
                copy.wait_recv()

        else:
            copy.wait_recv()
    back = ret[...].reshape(ne * cap, feat)
    total = jnp.zeros((tokens_n, feat), F32)
    for i in range(3):
        total += lax.dot_general(comb[i], back, (((0,), (0,)), ((), ())), preferred_element_type=F32)
    out_ref[...] = total.astype(BF)
    for copy in sends:
        copy.wait_send()
    for kept, copy in own_sends:

        @pl.when(jnp.logical_not(kept))
        def _():
            copy.wait_send()


def solution(mesh):
    ne, nf, nt = mesh.shape["expert"], mesh.shape["fsdp"], mesh.shape["tensor"]
    nx = nt // 2

    def body(tokens, expert_ids, gate_probs, w_gate, w_up, w_down):
        rows, feat = tokens.shape
        width = w_gate.shape[2]
        half = width // 2
        cap = 3 * rows // ne
        per = cap // CH
        chunks = ne * per
        groups = chunks // nx
        cfg = dict(ne=ne, nf=nf, nx=nx, cap=cap, half=half, lag=0, tile=256 if width % 256 == 0 else 128)
        any_ = pl.BlockSpec(memory_space=pl.ANY)
        dma = pltpu.SemaphoreType.DMA
        piece = nx * CH // nf
        call = pl.pallas_call(
            functools.partial(kernel, cfg),
            out_shape=jax.ShapeDtypeStruct((rows, feat), BF),
            in_specs=[any_] * 6,
            out_specs=pl.BlockSpec(memory_space=pltpu.VMEM),
            scratch_shapes=[
                pltpu.VMEM((rows, feat), BF),
                pltpu.VMEM((2, rows), jnp.int32),
                pltpu.VMEM((2, rows), F32),
                pltpu.VMEM((2, feat, width), BF),
                pltpu.VMEM((width, feat), BF),
                pltpu.VMEM((ne, per, CH, feat), BF),
                pltpu.VMEM((3, ne * cap, rows), BF),
                pltpu.VMEM((2, chunks, CH, feat), BF),
                pltpu.VMEM((chunks, CH, width), F32),
                pltpu.VMEM((groups, nx - 1, CH, width), BF),
                pltpu.VMEM((groups, nx - 1, CH, width), BF),
                pltpu.VMEM((2, chunks, CH, half), BF),
                pltpu.VMEM((groups, nf, piece, feat), F32),
                pltpu.VMEM((ne, cap // piece, piece, feat), BF),
                pltpu.VMEM((groups, nf, piece, feat), F32),
                pltpu.VMEM((groups, piece, feat), BF),
                dma((6,)),
                dma((2,)), dma((2,)),
                dma((ne,)), dma((ne,)),
                dma((ne,)), dma((ne,)),
                dma((groups * (nx - 1),)), dma((groups * (nx - 1),)),
                dma((groups * (nx - 1),)), dma((groups * (nx - 1),)),
                dma((groups * nx,)), dma((groups * nx,)),
                dma((groups * nf,)), dma((groups * nf,)),
                dma((groups * nf,)), dma((groups * nf,)),
            ],
            compiler_params=pltpu.CompilerParams(
                collective_id=0, has_side_effects=True, vmem_limit_bytes=60 << 20
            ),
        )
        return call(tokens, expert_ids.T, gate_probs.T, w_gate[0], w_up[0], w_down[0])

    return jax.shard_map(
        body,
        mesh=mesh,
        in_specs=(
            P("expert", "tensor"),
            P("expert", None),
            P("expert", None),
            P("expert", "tensor", "fsdp"),
            P("expert", "tensor", "fsdp"),
            P("expert", "fsdp", "tensor"),
        ),
        out_specs=P("expert", "tensor"),
        check_vma=False,
    )
```

```python
import functools

import jax
import jax.numpy as jnp
from jax import lax
from jax.experimental import pallas as pl
from jax.experimental.pallas import tpu as pltpu
from jax.sharding import PartitionSpec as P

MESH = pl.DeviceIdType.MESH
CH = 16
BF = jnp.bfloat16
F32 = jnp.float32


def kernel(
    cfg,
    tok_hbm, ids_hbm, prob_hbm, wg_hbm, wu_hbm, wd_hbm, out_ref,
    tok, ids, prob, wgu, wd, outg, comb, xs, part, sb, rb, hid, osb, ret, yrecv, fin,
    ld_sem, w_ss, w_rs, d_ss, d_rs, f_ss, f_rs, r_ss, r_rs, a_ss, a_rs, h_ss, h_rs, y1_ss, y1_rs, y2_ss, y2_rs,
):
    ne, nf, nx, cap = cfg["ne"], cfg["nf"], cfg["nx"], cfg["cap"]
    half = cfg["half"]
    per = cap // CH
    groups = ne * per // nx
    rows_y = nx * CH // nf
    in_block = cap // rows_y
    routes = []
    for way, reach in ((1, nx // 2), (-1, nx - 1 - nx // 2)):
        for d in range(reach, 1, -2):
            routes += [(way, d, "leaf"), (way, d - 1, "relay")]
        if reach % 2:
            routes.append((way, 1, "alone"))
    tokens_n = tok.shape[0]
    feat = tok.shape[1]

    z, y, t = lax.axis_index("expert"), lax.axis_index("fsdp"), lax.axis_index("tensor")
    x, c = t // 2, t % 2
    other = 1 - c
    sgn = 1 - 2 * c
    partner = (z, y, x * 2 + other)

    def at_x(k):
        return (x + sgn * k + 2 * nx) % nx

    def dev_x(k):
        return (z, y, at_x(k) * 2 + c)

    def dev_z(k):
        return ((z + k + ne) % ne, y, t)

    def dev_y(k):
        return (z, (y + k + nf) % nf, t)

    class Remote:
        def __init__(self, src, dst, ss, rs, dev):
            self.copy = pltpu.make_async_remote_copy(
                src_ref=src, dst_ref=dst, send_sem=ss, recv_sem=rs, device_id=dev, device_id_type=MESH
            )
            self.start, self.wait_send, self.waited = self.copy.start, self.copy.wait_send, False

        def wait_recv(self):
            if not self.waited:
                self.copy.wait_recv()
            self.waited = True

    remote = Remote
    sends = []

    mine = pl.ds(pl.multiple_of(c * half, 128), half)
    theirs = pl.ds(pl.multiple_of(other * half, 128), half)
    loads = [
        pltpu.make_async_copy(ids_hbm, ids, ld_sem.at[0]),
        pltpu.make_async_copy(prob_hbm, prob, ld_sem.at[1]),
        pltpu.make_async_copy(tok_hbm, tok, ld_sem.at[2]),
        pltpu.make_async_copy(wg_hbm.at[:, mine], wgu.at[c, :, 0:half], ld_sem.at[3]),
        pltpu.make_async_copy(wu_hbm.at[:, mine], wgu.at[c, :, half : 2 * half], ld_sem.at[4]),
        pltpu.make_async_copy(wd_hbm, wd, ld_sem.at[5]),
    ]
    for copy in loads:
        copy.start()

    barrier = pltpu.get_barrier_semaphore()
    peers = [partner]
    offsets = {way * d % nx for way, d, kind in routes if kind != "leaf"} | {way % nx for way, d, kind in routes}
    peers += [dev_x(k) for k in sorted(offsets | {-k % nx for k in offsets})]
    peers += [dev_z(k) for k in range(1, ne)]
    peers += [dev_y(k) for k in range(1, nf)]
    for peer in peers:
        pl.semaphore_signal(barrier, inc=1, device_id=peer, device_id_type=MESH)

    loads[0].wait()
    loads[1].wait()
    expert_row = lax.broadcasted_iota(jnp.int32, (ne, tokens_n), 0)
    first = expert_row == ids[0:1, :]
    second = expert_row == ids[1:2, :]
    named = jnp.where(first, 1.0, 0.0) + jnp.where(second, 1.0, 0.0)
    weight = jnp.where(first, prob[0:1, :], 0.0) + jnp.where(second, prob[1:2, :], 0.0)
    earlier = jnp.where(
        lax.broadcasted_iota(jnp.int32, (tokens_n, tokens_n), 0)
        < lax.broadcasted_iota(jnp.int32, (tokens_n, tokens_n), 1),
        1.0,
        0.0,
    ).astype(BF)
    rank = jnp.dot(named.astype(BF), earlier, preferred_element_type=F32)
    rank = jnp.where(named > 0.5, rank, -1.0)
    slot_row = lax.broadcasted_iota(jnp.int32, (cap, tokens_n), 0).astype(F32)
    hi = weight.astype(BF).astype(F32)
    mid = (weight - hi).astype(BF).astype(F32)
    low = weight - hi - mid
    loads[2].wait()
    for e in range(ne):
        chosen = slot_row == rank[e : e + 1, :]
        rows = jnp.dot(jnp.where(chosen, 1.0, 0.0).astype(BF), tok[...], preferred_element_type=F32)
        outg[e] = rows.astype(BF).reshape(per, CH, feat)
        for i, term in enumerate((hi, mid, low)):
            comb[i, e * cap : (e + 1) * cap, :] = jnp.where(chosen, term[e : e + 1, :], 0.0).astype(BF)

    pl.semaphore_wait(barrier, len(peers))

    swaps = [
        remote(wg_hbm.at[:, theirs], wgu.at[c, :, 0:half], w_ss.at[0], w_rs.at[0], partner),
        remote(wu_hbm.at[:, theirs], wgu.at[c, :, half : 2 * half], w_ss.at[1], w_rs.at[1], partner),
    ]
    for copy in swaps:
        copy.start()
        sends.append(copy)

    xs[c, 0:per] = outg[z]
    dispatch = [None]
    for p in range(1, ne):
        copy = remote(
            outg.at[(z - p + ne) % ne], xs.at[c, p * per : (p + 1) * per], d_ss.at[p], d_rs.at[p], dev_z(-p)
        )
        copy.start()
        dispatch.append(copy)
        sends.append(copy)

    handed = {}

    def hand(p):
        if p in handed:
            return
        if p > 0:
            dispatch[p].wait_recv()
        view = xs.at[c, p * per : (p + 1) * per]
        copy = remote(view, view, f_ss.at[p], f_rs.at[p], partner)
        copy.start()
        handed[p] = copy
        sends.append(copy)

    def blocks_of(g):
        return range(g * nx // per, ((g + 1) * nx - 1) // per + 1)

    taken = set()
    loaded = []

    def first_product(g):
        for p in blocks_of(g):
            hand(p)
        if not loaded:
            for copy in (loads[3], loads[4]):
                copy.wait()
            for copy in swaps:
                copy.wait_recv()
            loaded.append(1)
        for p in blocks_of(g):
            if p not in taken:
                handed[p].wait_recv()
                taken.add(p)
        a0 = xs[0, g * nx : (g + 1) * nx].reshape(nx * CH, feat)
        a1 = xs[1, g * nx : (g + 1) * nx].reshape(nx * CH, feat)
        tile = cfg["tile"]
        for n in range(2 * half // tile):
            cols = slice(n * tile, (n + 1) * tile)
            acc = jnp.dot(a0, wgu[0, :, cols], preferred_element_type=F32)
            acc += jnp.dot(a1, wgu[1, :, cols], preferred_element_type=F32)
            part[g * nx : (g + 1) * nx, :, cols] = acc.reshape(nx, CH, tile)

    got = {}

    def send_own(g, only):
        for i, (way, d, kind) in enumerate(routes):
            if kind != only:
                continue
            sb[g, i] = part[g * nx + at_x(way * d)].astype(BF)
            j = g * (nx - 1) + i
            copy = remote(sb.at[g, i], rb.at[g, i], r_ss.at[j], r_rs.at[j], dev_x(way))
            copy.start()
            got[g, i] = copy
            sends.append(copy)

    def relay_sends(g):
        for i, (way, d, kind) in enumerate(routes):
            if kind != "relay":
                continue
            k = routes.index((way, d + 1, "leaf"))
            value = part[g * nx + at_x(way * d)]
            got[g, k].wait_recv()
            sb[g, i] = (value + rb[g, k].astype(F32)).astype(BF)
            j = g * (nx - 1) + i
            copy = remote(sb.at[g, i], rb.at[g, i], r_ss.at[j], r_rs.at[j], dev_x(way * d))
            copy.start()
            got[g, i] = copy
            sends.append(copy)
        send_own(g, "alone")

    given = {}

    def give(g, owner, n):
        view = hid.at[c, g * nx + owner]
        i = g * nx + n
        copy = remote(view, view, h_ss.at[i], h_rs.at[i], partner)
        copy.start()
        given[g, n] = copy
        sends.append(copy)

    def finish(g):
        value = part[g * nx + x]
        for i, (way, d, kind) in enumerate(routes):
            if kind != "leaf":
                got[g, i].wait_recv()
                value = value + rb[g, i].astype(F32)
        gate, up = value[:, :half], value[:, half:]
        hid[c, g * nx + x] = (gate / (1.0 + jnp.exp(-gate)) * up).astype(BF)
        for i, (way, d, kind) in enumerate(routes):
            if kind != "leaf":
                spread(g, i, x, way * d)
        give(g, x, nx - 1)

    shared = {}

    def spread(g, i, owner, to):
        view = hid.at[c, g * nx + owner]
        j = g * (nx - 1) + i
        copy = remote(view, view, a_ss.at[j], a_rs.at[j], dev_x(to))
        copy.start()
        shared[g, i] = copy
        sends.append(copy)

    def relay_hidden(g):
        for i, (way, d, kind) in enumerate(routes):
            if kind == "leaf":
                continue
            shared[g, i].wait_recv()
            owner = at_x(-way * d)
            if kind == "relay":
                spread(g, routes.index((way, d + 1, "leaf")), owner, way)
            give(g, owner, i)

    def collect_hidden(g):
        for i, (way, d, kind) in enumerate(routes):
            if kind == "leaf":
                shared[g, i].wait_recv()
                give(g, at_x(-way * d), i)

    summed, cast = {}, {}

    def second_product(g):
        if g == 0:
            loads[5].wait()
        for n in range(nx):
            given[g, n].wait_recv()
        h0 = hid[0, g * nx : (g + 1) * nx].reshape(nx * CH, half)
        h1 = hid[1, g * nx : (g + 1) * nx].reshape(nx * CH, half)
        value = jnp.dot(h0, wd[0:half, :], preferred_element_type=F32)
        value += jnp.dot(h1, wd[half : 2 * half, :], preferred_element_type=F32)
        osb[g] = value.reshape(nf, rows_y, feat)
        for k in range(1, nf):
            i = g * nf + k
            copy = remote(osb.at[g, (y + k) % nf], yrecv.at[g, k], y1_ss.at[i], y1_rs.at[i], dev_y(k))
            copy.start()
            summed[g, k] = copy
            sends.append(copy)

    def send_back(g):
        value = osb[g, y]
        for k in range(1, nf):
            summed[g, k].wait_recv()
            value = value + yrecv[g, k]
        fin[g] = value.astype(BF)
        q = g * nf + y
        home = q // in_block
        place = ret.at[z, q % in_block]
        to_z = (z + home) % ne
        for k in range(nf):
            i = g * nf + k
            copy = remote(fin.at[g], place, y2_ss.at[i], y2_rs.at[q], (to_z, (y + k) % nf, t))
            if k == 0 and g * nf < in_block:
                kept = q < in_block

                @pl.when(kept)
                def _():
                    ret[z, q % in_block] = fin[g]

                @pl.when(jnp.logical_not(kept))
                def _():
                    copy.start()

                own_sends.append((kept, copy))
            else:
                copy.start()
                sends.append(copy)

    own_sends = []
    stages = [
        lambda g: (first_product(g), send_own(g, "leaf")), relay_sends, finish, relay_hidden, collect_hidden, second_product, send_back,
    ]
    start, pace = (0, 3, 5, 8, 11, 14, 18), (1, 1.6, 2, 2, 2, 1.6, 1)
    for _, n, g in sorted((start[n] + pace[n] * g, n, g) for n in range(len(stages)) for g in range(groups)):
        stages[n](g)

    for q in range(groups * nf):
        copy = remote(fin.at[0], ret.at[0, 0], y2_ss.at[0], y2_rs.at[q], partner)
        if q < in_block:

            @pl.when(y != q % nf)
            def _():
                copy.wait_recv()

        else:
            copy.wait_recv()
    back = ret[...].reshape(ne * cap, feat)
    total = jnp.zeros((tokens_n, feat), F32)
    for i in range(3):
        total += lax.dot_general(comb[i], back, (((0,), (0,)), ((), ())), preferred_element_type=F32)
    out_ref[...] = total.astype(BF)
    for copy in sends:
        copy.wait_send()
    for kept, copy in own_sends:

        @pl.when(jnp.logical_not(kept))
        def _():
            copy.wait_send()


def solution(mesh):
    ne, nf, nt = mesh.shape["expert"], mesh.shape["fsdp"], mesh.shape["tensor"]
    nx = nt // 2

    def body(tokens, expert_ids, gate_probs, w_gate, w_up, w_down):
        rows, feat = tokens.shape
        width = w_gate.shape[2]
        half = width // 2
        cap = 3 * rows // ne
        per = cap // CH
        chunks = ne * per
        groups = chunks // nx
        cfg = dict(ne=ne, nf=nf, nx=nx, cap=cap, half=half, tile=256 if width % 256 == 0 else 128)
        any_ = pl.BlockSpec(memory_space=pl.ANY)
        dma = pltpu.SemaphoreType.DMA
        piece = nx * CH // nf
        call = pl.pallas_call(
            functools.partial(kernel, cfg),
            out_shape=jax.ShapeDtypeStruct((rows, feat), BF),
            in_specs=[any_] * 6,
            out_specs=pl.BlockSpec(memory_space=pltpu.VMEM),
            scratch_shapes=[
                pltpu.VMEM((rows, feat), BF),
                pltpu.VMEM((2, rows), jnp.int32),
                pltpu.VMEM((2, rows), F32),
                pltpu.VMEM((2, feat, width), BF),
                pltpu.VMEM((width, feat), BF),
                pltpu.VMEM((ne, per, CH, feat), BF),
                pltpu.VMEM((3, ne * cap, rows), BF),
                pltpu.VMEM((2, chunks, CH, feat), BF),
                pltpu.VMEM((chunks, CH, width), F32),
                pltpu.VMEM((groups, nx - 1, CH, width), BF),
                pltpu.VMEM((groups, nx - 1, CH, width), BF),
                pltpu.VMEM((2, chunks, CH, half), BF),
                pltpu.VMEM((groups, nf, piece, feat), F32),
                pltpu.VMEM((ne, cap // piece, piece, feat), BF),
                pltpu.VMEM((groups, nf, piece, feat), F32),
                pltpu.VMEM((groups, piece, feat), BF),
                dma((6,)),
                dma((2,)), dma((2,)),
                dma((ne,)), dma((ne,)),
                dma((ne,)), dma((ne,)),
                dma((groups * (nx - 1),)), dma((groups * (nx - 1),)),
                dma((groups * (nx - 1),)), dma((groups * (nx - 1),)),
                dma((groups * nx,)), dma((groups * nx,)),
                dma((groups * nf,)), dma((groups * nf,)),
                dma((groups * nf,)), dma((groups * nf,)),
            ],
            compiler_params=pltpu.CompilerParams(
                collective_id=0, has_side_effects=True, vmem_limit_bytes=60 << 20
            ),
        )
        return call(tokens, expert_ids.T, gate_probs.T, w_gate[0], w_up[0], w_down[0])

    return jax.shard_map(
        body,
        mesh=mesh,
        in_specs=(
            P("expert", "tensor"),
            P("expert", None),
            P("expert", None),
            P("expert", "tensor", "fsdp"),
            P("expert", "tensor", "fsdp"),
            P("expert", "fsdp", "tensor"),
        ),
        out_specs=P("expert", "tensor"),
        check_vma=False,
    )
```

```python
import functools

import jax
import jax.numpy as jnp
from jax import lax
from jax.experimental import pallas as pl
from jax.experimental.pallas import tpu as pltpu
from jax.sharding import PartitionSpec as P

MESH = pl.DeviceIdType.MESH
CH = 16
BF = jnp.bfloat16
F32 = jnp.float32


def kernel(
    cfg,
    tok_hbm, ids_hbm, prob_hbm, wg_hbm, wu_hbm, wd_hbm, out_ref,
    tok, ids, prob, wgu, wd, outg, comb, xs, part, sb, rb, hid, osb, ret, yrecv, fin,
    ld_sem, w_ss, w_rs, d_ss, d_rs, f_ss, f_rs, r_ss, r_rs, a_ss, a_rs, h_ss, h_rs, y1_ss, y1_rs, y2_ss, y2_rs,
):
    ne, nf, nx, cap = cfg["ne"], cfg["nf"], cfg["nx"], cfg["cap"]
    half = cfg["half"]
    per = cap // CH
    groups = ne * per // nx
    rows_y = nx * CH // nf
    in_block = cap // rows_y
    routes = []
    for way, reach in ((1, nx // 2), (-1, nx - 1 - nx // 2)):
        for d in range(reach, 1, -2):
            routes += [(way, d, "leaf"), (way, d - 1, "relay")]
        if reach % 2:
            routes.append((way, 1, "alone"))
    tokens_n = tok.shape[0]
    feat = tok.shape[1]

    z, y, t = lax.axis_index("expert"), lax.axis_index("fsdp"), lax.axis_index("tensor")
    x, c = t // 2, t % 2
    other = 1 - c
    sgn = 1 - 2 * c
    partner = (z, y, x * 2 + other)

    def at_x(k):
        return (x + sgn * k + 2 * nx) % nx

    def dev_x(k):
        return (z, y, at_x(k) * 2 + c)

    def dev_z(k):
        return ((z + k + ne) % ne, y, t)

    def dev_y(k):
        return (z, (y + k + nf) % nf, t)

    class Remote:
        def __init__(self, src, dst, ss, rs, dev):
            self.copy = pltpu.make_async_remote_copy(
                src_ref=src, dst_ref=dst, send_sem=ss, recv_sem=rs, device_id=dev, device_id_type=MESH
            )
            self.start, self.wait_send, self.waited = self.copy.start, self.copy.wait_send, False

        def wait_recv(self):
            if not self.waited:
                self.copy.wait_recv()
            self.waited = True

    remote = Remote
    sends = []

    mine = pl.ds(pl.multiple_of(c * half, 128), half)
    theirs = pl.ds(pl.multiple_of(other * half, 128), half)
    loads = [
        pltpu.make_async_copy(ids_hbm, ids, ld_sem.at[0]),
        pltpu.make_async_copy(prob_hbm, prob, ld_sem.at[1]),
        pltpu.make_async_copy(tok_hbm, tok, ld_sem.at[2]),
        pltpu.make_async_copy(wg_hbm.at[:, mine], wgu.at[c, :, 0:half], ld_sem.at[3]),
        pltpu.make_async_copy(wu_hbm.at[:, mine], wgu.at[c, :, half : 2 * half], ld_sem.at[4]),
        pltpu.make_async_copy(wd_hbm, wd, ld_sem.at[5]),
    ]
    for copy in loads:
        copy.start()

    barrier = pltpu.get_barrier_semaphore()
    peers = [partner]
    offsets = {way * d % nx for way, d, kind in routes if kind != "leaf"} | {way % nx for way, d, kind in routes}
    peers += [dev_x(k) for k in sorted(offsets | {-k % nx for k in offsets})]
    peers += [dev_z(k) for k in range(1, ne)]
    peers += [dev_y(k) for k in range(1, nf)]
    for peer in peers:
        pl.semaphore_signal(barrier, inc=1, device_id=peer, device_id_type=MESH)

    loads[0].wait()
    loads[1].wait()
    expert_row = lax.broadcasted_iota(jnp.int32, (ne, tokens_n), 0)
    first = expert_row == ids[0:1, :]
    second = expert_row == ids[1:2, :]
    named = jnp.where(first, 1.0, 0.0) + jnp.where(second, 1.0, 0.0)
    weight = jnp.where(first, prob[0:1, :], 0.0) + jnp.where(second, prob[1:2, :], 0.0)
    earlier = jnp.where(
        lax.broadcasted_iota(jnp.int32, (tokens_n, tokens_n), 0)
        < lax.broadcasted_iota(jnp.int32, (tokens_n, tokens_n), 1),
        1.0,
        0.0,
    ).astype(BF)
    rank = jnp.dot(named.astype(BF), earlier, preferred_element_type=F32)
    rank = jnp.where(named > 0.5, rank, -1.0)
    slot_row = lax.broadcasted_iota(jnp.int32, (cap, tokens_n), 0).astype(F32)
    hi = weight.astype(BF).astype(F32)
    mid = (weight - hi).astype(BF).astype(F32)
    low = weight - hi - mid
    loads[2].wait()
    for e in range(ne):
        chosen = slot_row == rank[e : e + 1, :]
        rows = jnp.dot(jnp.where(chosen, 1.0, 0.0).astype(BF), tok[...], preferred_element_type=F32)
        outg[e] = rows.astype(BF).reshape(per, CH, feat)
        for i, term in enumerate((hi, mid, low)):
            comb[i, e * cap : (e + 1) * cap, :] = jnp.where(chosen, term[e : e + 1, :], 0.0).astype(BF)

    pl.semaphore_wait(barrier, len(peers))

    swaps = [
        remote(wg_hbm.at[:, theirs], wgu.at[c, :, 0:half], w_ss.at[0], w_rs.at[0], partner),
        remote(wu_hbm.at[:, theirs], wgu.at[c, :, half : 2 * half], w_ss.at[1], w_rs.at[1], partner),
    ]
    for copy in swaps:
        copy.start()
        sends.append(copy)

    xs[c, 0:per] = outg[z]
    dispatch = [None]
    for p in range(1, ne):
        copy = remote(
            outg.at[(z - p + ne) % ne], xs.at[c, p * per : (p + 1) * per], d_ss.at[p], d_rs.at[p], dev_z(-p)
        )
        copy.start()
        dispatch.append(copy)
        sends.append(copy)

    handed = {}

    def hand(p):
        if p in handed:
            return
        if p > 0:
            dispatch[p].wait_recv()
        view = xs.at[c, p * per : (p + 1) * per]
        copy = remote(view, view, f_ss.at[p], f_rs.at[p], partner)
        copy.start()
        handed[p] = copy
        sends.append(copy)

    def blocks_of(g):
        return range(g * nx // per, ((g + 1) * nx - 1) // per + 1)

    taken = set()
    loaded = []

    def first_product(g):
        for p in blocks_of(g) if g == 0 else range(ne):
            hand(p)
        if not loaded:
            for copy in (loads[3], loads[4]):
                copy.wait()
            for copy in swaps:
                copy.wait_recv()
            loaded.append(1)
        for p in blocks_of(g):
            if p not in taken:
                handed[p].wait_recv()
                taken.add(p)
        a0 = xs[0, g * nx : (g + 1) * nx].reshape(nx * CH, feat)
        a1 = xs[1, g * nx : (g + 1) * nx].reshape(nx * CH, feat)
        tile = cfg["tile"]
        for n in range(2 * half // tile):
            cols = slice(n * tile, (n + 1) * tile)
            acc = jnp.dot(a0, wgu[0, :, cols], preferred_element_type=F32)
            acc += jnp.dot(a1, wgu[1, :, cols], preferred_element_type=F32)
            part[g * nx : (g + 1) * nx, :, cols] = acc.reshape(nx, CH, tile)

    got = {}

    def send_own(g, only):
        for i, (way, d, kind) in enumerate(routes):
            if kind != only:
                continue
            sb[g, i] = part[g * nx + at_x(way * d)].astype(BF)
            j = g * (nx - 1) + i
            copy = remote(sb.at[g, i], rb.at[g, i], r_ss.at[j], r_rs.at[j], dev_x(way))
            copy.start()
            got[g, i] = copy
            sends.append(copy)

    def relay_sends(g):
        for i, (way, d, kind) in enumerate(routes):
            if kind != "relay":
                continue
            k = routes.index((way, d + 1, "leaf"))
            value = part[g * nx + at_x(way * d)]
            got[g, k].wait_recv()
            sb[g, i] = (value + rb[g, k].astype(F32)).astype(BF)
            j = g * (nx - 1) + i
            copy = remote(sb.at[g, i], rb.at[g, i], r_ss.at[j], r_rs.at[j], dev_x(way * d))
            copy.start()
            got[g, i] = copy
            sends.append(copy)
        send_own(g, "alone")

    given = {}

    def give(g, owner, n):
        view = hid.at[c, g * nx + owner]
        i = g * nx + n
        copy = remote(view, view, h_ss.at[i], h_rs.at[i], partner)
        copy.start()
        given[g, n] = copy
        sends.append(copy)

    def finish(g):
        value = part[g * nx + x]
        for i, (way, d, kind) in enumerate(routes):
            if kind != "leaf":
                got[g, i].wait_recv()
                value = value + rb[g, i].astype(F32)
        gate, up = value[:, :half], value[:, half:]
        hid[c, g * nx + x] = (gate / (1.0 + jnp.exp(-gate)) * up).astype(BF)
        for i, (way, d, kind) in enumerate(routes):
            if kind != "leaf":
                spread(g, i, x, way * d)
        give(g, x, nx - 1)

    shared = {}

    def spread(g, i, owner, to):
        view = hid.at[c, g * nx + owner]
        j = g * (nx - 1) + i
        copy = remote(view, view, a_ss.at[j], a_rs.at[j], dev_x(to))
        copy.start()
        shared[g, i] = copy
        sends.append(copy)

    def relay_hidden(g):
        for i, (way, d, kind) in enumerate(routes):
            if kind == "leaf":
                continue
            shared[g, i].wait_recv()
            owner = at_x(-way * d)
            if kind == "relay":
                spread(g, routes.index((way, d + 1, "leaf")), owner, way)
            give(g, owner, i)

    def collect_hidden(g):
        for i, (way, d, kind) in enumerate(routes):
            if kind == "leaf":
                shared[g, i].wait_recv()
                give(g, at_x(-way * d), i)

    summed, cast = {}, {}

    def second_product(g):
        if g == 0:
            loads[5].wait()
        for n in range(nx):
            given[g, n].wait_recv()
        h0 = hid[0, g * nx : (g + 1) * nx].reshape(nx * CH, half)
        h1 = hid[1, g * nx : (g + 1) * nx].reshape(nx * CH, half)
        value = jnp.dot(h0, wd[0:half, :], preferred_element_type=F32)
        value += jnp.dot(h1, wd[half : 2 * half, :], preferred_element_type=F32)
        osb[g] = value.reshape(nf, rows_y, feat)
        for k in range(1, nf):
            i = g * nf + k
            copy = remote(osb.at[g, (y + k) % nf], yrecv.at[g, k], y1_ss.at[i], y1_rs.at[i], dev_y(k))
            copy.start()
            summed[g, k] = copy
            sends.append(copy)

    def send_back(g):
        value = osb[g, y]
        for k in range(1, nf):
            summed[g, k].wait_recv()
            value = value + yrecv[g, k]
        fin[g] = value.astype(BF)
        q = g * nf + y
        home = q // in_block
        place = ret.at[z, q % in_block]
        to_z = (z + home) % ne
        for k in range(nf):
            i = g * nf + k
            copy = remote(fin.at[g], place, y2_ss.at[i], y2_rs.at[q], (to_z, (y + k) % nf, t))
            if k == 0 and g * nf < in_block:
                kept = q < in_block

                @pl.when(kept)
                def _():
                    ret[z, q % in_block] = fin[g]

                @pl.when(jnp.logical_not(kept))
                def _():
                    copy.start()

                own_sends.append((kept, copy))
            else:
                copy.start()
                sends.append(copy)

    own_sends = []
    stages = [
        lambda g: (first_product(g), send_own(g, "leaf")), relay_sends, finish, relay_hidden, collect_hidden, second_product, send_back,
    ]
    start, pace = (0, 3, 5, 8, 11, 14, 18), (1, 1.6, 2, 2, 2, 1.6, 1)
    for _, n, g in sorted((start[n] + pace[n] * g, n, g) for n in range(len(stages)) for g in range(groups)):
        stages[n](g)

    for q in range(groups * nf):
        copy = remote(fin.at[0], ret.at[0, 0], y2_ss.at[0], y2_rs.at[q], partner)
        if q < in_block:

            @pl.when(y != q % nf)
            def _():
                copy.wait_recv()

        else:
            copy.wait_recv()
    back = ret[...].reshape(ne * cap, feat)
    total = jnp.zeros((tokens_n, feat), F32)
    for i in range(3):
        total += lax.dot_general(comb[i], back, (((0,), (0,)), ((), ())), preferred_element_type=F32)
    out_ref[...] = total.astype(BF)
    for copy in sends:
        copy.wait_send()
    for kept, copy in own_sends:

        @pl.when(jnp.logical_not(kept))
        def _():
            copy.wait_send()


def solution(mesh):
    ne, nf, nt = mesh.shape["expert"], mesh.shape["fsdp"], mesh.shape["tensor"]
    nx = nt // 2

    def body(tokens, expert_ids, gate_probs, w_gate, w_up, w_down):
        rows, feat = tokens.shape
        width = w_gate.shape[2]
        half = width // 2
        cap = 3 * rows // ne
        per = cap // CH
        chunks = ne * per
        groups = chunks // nx
        cfg = dict(ne=ne, nf=nf, nx=nx, cap=cap, half=half, tile=256 if width % 256 == 0 else 128)
        any_ = pl.BlockSpec(memory_space=pl.ANY)
        dma = pltpu.SemaphoreType.DMA
        piece = nx * CH // nf
        call = pl.pallas_call(
            functools.partial(kernel, cfg),
            out_shape=jax.ShapeDtypeStruct((rows, feat), BF),
            in_specs=[any_] * 6,
            out_specs=pl.BlockSpec(memory_space=pltpu.VMEM),
            scratch_shapes=[
                pltpu.VMEM((rows, feat), BF),
                pltpu.VMEM((2, rows), jnp.int32),
                pltpu.VMEM((2, rows), F32),
                pltpu.VMEM((2, feat, width), BF),
                pltpu.VMEM((width, feat), BF),
                pltpu.VMEM((ne, per, CH, feat), BF),
                pltpu.VMEM((3, ne * cap, rows), BF),
                pltpu.VMEM((2, chunks, CH, feat), BF),
                pltpu.VMEM((chunks, CH, width), F32),
                pltpu.VMEM((groups, nx - 1, CH, width), BF),
                pltpu.VMEM((groups, nx - 1, CH, width), BF),
                pltpu.VMEM((2, chunks, CH, half), BF),
                pltpu.VMEM((groups, nf, piece, feat), F32),
                pltpu.VMEM((ne, cap // piece, piece, feat), BF),
                pltpu.VMEM((groups, nf, piece, feat), F32),
                pltpu.VMEM((groups, piece, feat), BF),
                dma((6,)),
                dma((2,)), dma((2,)),
                dma((ne,)), dma((ne,)),
                dma((ne,)), dma((ne,)),
                dma((groups * (nx - 1),)), dma((groups * (nx - 1),)),
                dma((groups * (nx - 1),)), dma((groups * (nx - 1),)),
                dma((groups * nx,)), dma((groups * nx,)),
                dma((groups * nf,)), dma((groups * nf,)),
                dma((groups * nf,)), dma((groups * nf,)),
            ],
            compiler_params=pltpu.CompilerParams(
                collective_id=0, has_side_effects=True, vmem_limit_bytes=60 << 20
            ),
        )
        return call(tokens, expert_ids.T, gate_probs.T, w_gate[0], w_up[0], w_down[0])

    return jax.shard_map(
        body,
        mesh=mesh,
        in_specs=(
            P("expert", "tensor"),
            P("expert", None),
            P("expert", None),
            P("expert", "tensor", "fsdp"),
            P("expert", "tensor", "fsdp"),
            P("expert", "fsdp", "tensor"),
        ),
        out_specs=P("expert", "tensor"),
        check_vma=False,
    )
```
